32 devices in a mesh: ctx: 16 (over z, y, x), tp: 2 (over core).
Axes of the slice: x: 2, y: 2, z: 4, core: 2. Of those that a mesh axis runs over, the one named last changes fastest.
Arguments:
- queries: bfloat16 [4096, 8192], P('ctx', 'tp'), may hold values from -8 to 8
- span_kv: bfloat16 [4096, 8, 2, 128], P('ctx', 'tp'), may hold values from -8 to 8
- cache_kv: bfloat16 [8192, 8, 2, 128], P('ctx', 'tp'), may hold values from -4 to 4
- out_weight: bfloat16 [8192, 8192], P('tp', 'ctx'), may hold values from -2.390625 to 2.390625
- offset: int32 [1], replicated, may hold values from 8192 to 16383
- lengths: int32 [32], replicated, may hold values from 64 to 256, as said below
Outputs:
- mixed: bfloat16 [4096, 8192], P('tp', 'ctx')
The draws below stay inside these ranges and needn't reach their ends.
Inputs may be any that keep to these rules, and one draw needn't show every extreme that they name: `lengths`: each at most 256; in every draw some match has all 256 of its positions valid.
All inputs are finite; a program needn't handle non-finite values.
Results may differ from the reference program's by a relative error of at most 0.025.
Values may be sent and summed in bfloat16 or wider, within the bound.
No kernel may reach another device: no remote copies, remote signals or barrier semaphores. Data moves between devices by JAX's collectives and lax.ppermute only.
A program may use at most 192 MiB of HBM per device.

```python
import math
import jax
import jax.numpy as jnp
from jax import lax

D = 8192
HEADS = 64
KV_HEADS = 8
HEAD_DIM = 128
TOKENS = 4096
SLOT = 256
CACHE = 8192
MATCHES = 32


def draw_queries(key, part):
    base_key = jax.random.fold_in(key, 11)
    shape = (TOKENS, HEADS, HEAD_DIM)
    entries = jnp.clip(2.0 * jax.random.normal(base_key, shape, jnp.float32), -8.0, 8.0)
    return entries.reshape(TOKENS, HEADS * HEAD_DIM).astype(jnp.bfloat16)


def draw_span_kv(key, part):
    base_key = jax.random.fold_in(key, 12)
    shape = (TOKENS, KV_HEADS, 2, HEAD_DIM)
    entries = jnp.clip(jax.random.normal(base_key, shape, jnp.float32), -4.0, 4.0)
    return entries.astype(jnp.bfloat16)


def draw_lengths(key, part):
    counts = jax.random.randint(jax.random.fold_in(key, 21), (MATCHES,), SLOT // 4, SLOT + 1)
    filled = jax.random.randint(jax.random.fold_in(key, 22), (), 0, MATCHES)
    return jnp.where(jnp.arange(MATCHES) == filled, SLOT, counts).astype(jnp.int32)


def block_levels(rng, dims, split, least, high):
    def one(dim, shards_of):
        heights = jax.random.uniform(jax.random.fold_in(jax.random.fold_in(rng, 6), dim), (shards_of,), jnp.float32, least / len(split), high / len(split))
        return jnp.repeat(jnp.exp(heights), dims[dim] // shards_of).reshape((-1,) + (1,) * (len(dims) - dim - 1))

    level = one(*split[0])
    for cut in split[1:]:
        level = level * one(*cut)
    return level


def bell_draw(key, extent, spread, most, cuts=(), held_as=jnp.bfloat16):
    result = jax.random.normal(key, extent, jnp.float32) * spread
    if len(cuts) > 0:
        result = block_levels(key, extent, cuts, -0.22, 0.18) * result
    return jnp.clip(result, min=-most, max=most).astype(held_as)


def setup_inputs(seed: int = 0) -> dict:
    seeds = jax.random.split(jax.random.key(seed), 7)
    return {
        "queries": draw_queries(jax.random.fold_in(seeds[6], 71), 0),
        "span_kv": draw_span_kv(jax.random.fold_in(seeds[6], 71), 0),
        "cache_kv": bell_draw(seeds[2], (CACHE, KV_HEADS, 2, HEAD_DIM), 1.0, 4.0, ((0, 16), (1, 2))),
        "out_weight": bell_draw(seeds[3], (HEADS * HEAD_DIM, D), 0.4, 2.390625, ((0, 2), (1, 16))),
        "offset": jax.random.randint(seeds[4], (1,), CACHE, CACHE + 8192).astype(jnp.int32),
        "lengths": draw_lengths(jax.random.fold_in(seeds[6], 71), 0),
    }


lowest_score = -1e+30
rope_base = 500000.0

def rotate(values, positions):
    head_size = values.shape[-1]
    half_dim = head_size // 2
    frequency = jnp.exp(jnp.arange(half_dim, dtype=jnp.float32) * (-2.0 * math.log(rope_base) / head_size))
    angles = positions.astype(jnp.float32)[:, None] * frequency[None, :]
    cosine = jnp.cos(angles)[:, None, :]
    sine_part = jnp.sin(angles)[:, None, :]
    first_half = values[..., :half_dim]
    second_half = values[..., half_dim:]
    return jnp.concatenate([first_half * cosine - second_half * sine_part, second_half * cosine + first_half * sine_part], axis=-1)

def reference(queries, span_kv, cache_kv, out_weight, offset, lengths):
    group = HEADS // KV_HEADS
    scale = 1.0 / math.sqrt(HEAD_DIM)
    positions = offset[0] + jnp.arange(TOKENS, dtype=jnp.int32)
    rotated = rotate(queries.reshape(TOKENS, HEADS, HEAD_DIM).astype(jnp.float32), positions).astype(jnp.bfloat16)
    rotated = rotated.reshape(TOKENS, KV_HEADS, group, HEAD_DIM)
    span_keys = rotate(span_kv[:, :, 0, :].astype(jnp.float32), positions).astype(jnp.bfloat16)
    every_key = jnp.concatenate([cache_kv[:, :, 0, :], span_keys], axis=0).astype(jnp.float32)
    every_value = jnp.concatenate([cache_kv[:, :, 1, :], span_kv[:, :, 1, :]], axis=0).astype(jnp.float32)
    cache_index = jnp.arange(CACHE, dtype=jnp.int32)
    cache_valid = cache_index % SLOT < lengths[cache_index // SLOT]
    span_index = jnp.arange(TOKENS, dtype=jnp.int32)
    block = min(TOKENS, 256)
    block_count = TOKENS // block

    def one_block(index):
        row_block = index // KV_HEADS
        head = index % KV_HEADS
        query_part = lax.dynamic_slice_in_dim(rotated, (row_block * block).astype(jnp.int32), block, 0)
        query_part = lax.dynamic_index_in_dim(query_part, head, axis=1, keepdims=False).astype(jnp.float32)
        key_rows = lax.dynamic_index_in_dim(every_key, head, axis=1, keepdims=False)
        value_rows = lax.dynamic_index_in_dim(every_value, head, axis=1, keepdims=False)
        scores = jnp.einsum('tgd,nd->tgn', query_part, key_rows) * scale
        query_token = row_block * block + jnp.arange(block, dtype=jnp.int32)
        span_valid = span_index[None, :] <= query_token[:, None]
        valid = jnp.concatenate([jnp.broadcast_to(cache_valid[None, :], (block, CACHE)), span_valid], axis=1)[:, None, :]
        scores = jnp.where(valid, scores, lowest_score)
        row_max = lax.optimization_barrier(jnp.max(scores, axis=-1, keepdims=True))
        weights = jnp.where(valid, jnp.exp(scores - row_max), 0.0)
        denominators = lax.optimization_barrier(jnp.sum(weights, axis=-1))
        rounded = lax.optimization_barrier(weights.astype(jnp.bfloat16)).astype(jnp.float32)
        numerator = jnp.einsum('tgn,nd->tgd', rounded, value_rows)
        return (numerator / denominators[..., None]).astype(jnp.bfloat16)
    blocks = lax.map(one_block, jnp.arange(block_count * KV_HEADS, dtype=jnp.int32))
    attention = blocks.reshape(block_count, KV_HEADS, block, group, HEAD_DIM).transpose(0, 2, 1, 3, 4)
    attention = attention.reshape(TOKENS, HEADS * HEAD_DIM)
    return jnp.dot(attention, out_weight, preferred_element_type=jnp.float32).astype(jnp.bfloat16)
```

```python
import functools
import math

import jax
import jax.numpy as jnp
from jax import lax
from jax.experimental import pallas as pl
from jax.experimental.pallas import tpu as pltpu
from jax.sharding import Mesh
from jax.sharding import PartitionSpec as P


F32 = jnp.float32
BF16 = jnp.bfloat16
lowest_score = -1e30
rope_base = 500000.0
bound_limit = 90.0
key_rows = 512


def rotate(values, positions):
    head_size = values.shape[-1]
    half_dim = head_size // 2
    frequency = jnp.exp(
        jnp.arange(half_dim, dtype=F32) * (-2.0 * math.log(rope_base) / head_size)
    )
    angles = positions.astype(F32)[:, None] * frequency[None, :]
    cosine = jnp.cos(angles)[:, None, :]
    sine_part = jnp.sin(angles)[:, None, :]
    first_half = values[..., :half_dim]
    second_half = values[..., half_dim:]
    return jnp.concatenate(
        [
            first_half * cosine - second_half * sine_part,
            second_half * cosine + first_half * sine_part,
        ],
        axis=-1,
    )


def square_bound(rows):
    squares = (rows * rows).astype(BF16)
    ones = jnp.ones((rows.shape[1], rows.shape[1]), BF16)
    sums = jnp.dot(squares, ones, preferred_element_type=F32)
    return jnp.max(sums, axis=0, keepdims=True)


def attend(queries, entries, lengths, j, start, stride):
    chunks, rows, width = queries.shape
    count = chunks // stride
    nj, nz, local, pair = entries.shape
    head = pair // 2
    group = width // head
    cached = local - rows
    shards = nj * nz
    slots = lengths.shape[0]
    slot = cached * shards // slots
    per_shard = cached // slot
    span = shards * rows
    block = key_rows
    span_blocks = span // block
    stack = group * rows
    scale = math.log2(math.e) / math.sqrt(head)
    capacity = span + shards * cached + block

    def kernel(meta_ref, len_ref, q_ref, kv_ref, o_ref, keys, values, stacked, acc, top, norms, counts, bounds):
        step = pl.program_id(0)

        @pl.when(step == 0)
        def _():
            norms[...] = jnp.zeros_like(norms)

            def put_span(shard, carry):
                place = pl.ds(pl.multiple_of(shard * rows, rows), rows)
                piece = kv_ref[shard % nj, shard // nj, pl.ds(cached, rows), :]
                keys[place, :] = piece[:, :head]
                values[place, :head] = piece[:, head:]
                values[place, head:] = jnp.ones((rows, head), BF16)
                norms[...] = jnp.maximum(norms[...], square_bound(piece[:, :head].astype(F32)))
                return carry

            lax.fori_loop(0, shards, put_span, 0)
            index = lax.broadcasted_iota(jnp.int32, (slot, head), 0)

            def put_slot(number, at):
                shard = number // per_shard
                inside = pl.multiple_of((number % per_shard) * slot, slot)
                piece = kv_ref[shard % nj, shard // nj, pl.ds(inside, slot), :].astype(F32)
                size = len_ref[number]
                valid = index < size
                fixed = jnp.where(valid, piece[:, :head], piece[0:1, :head])
                place = pl.ds(pl.multiple_of(at, 16), slot)
                keys[place, :] = fixed.astype(BF16)
                values[place, :head] = jnp.where(valid, piece[:, head:], 0.0).astype(BF16)
                values[place, head:] = jnp.where(valid, 1.0, 0.0).astype(BF16)
                norms[...] = jnp.maximum(norms[...], square_bound(fixed))
                return at + (size + 15) // 16 * 16

            end = lax.fori_loop(0, slots, put_slot, span)
            place = pl.ds(pl.multiple_of(end, 16), block)
            keys[place, :] = jnp.broadcast_to(kv_ref[0, 0, 0:1, :head], (block, head))
            values[place, :] = jnp.zeros((block, pair), BF16)
            counts[0] = (end - span + block - 1) // block
            bounds[0] = jnp.max(norms[...])

        for g in range(group):
            stacked[g * rows : (g + 1) * rows, :] = q_ref[0, :, g * head : (g + 1) * head]
        acc[...] = jnp.zeros_like(acc)
        first_token = (meta_ref[0] + (meta_ref[1] + step * stride) * nj) * rows
        full = first_token // block
        total = full + counts[0]
        query_bound = jnp.max(square_bound(stacked[...].astype(F32)))
        safe = query_bound * bounds[0] * (1.05 * scale * scale) <= bound_limit * bound_limit

        def scores_of(at):
            raw = lax.dot_general(
                stacked[...],
                keys[pl.ds(at, block), :],
                (((1,), (1,)), ((), ())),
                preferred_element_type=F32,
            )
            return raw * scale

        token = first_token + lax.broadcasted_iota(jnp.int32, (stack, block), 0) % rows
        column = lax.broadcasted_iota(jnp.int32, (stack, block), 1)

        def place_of(i):
            return pl.multiple_of(jnp.where(i < full, i, span_blocks + i - full) * block, block)

        def add_plain(at, scores):
            weights = jnp.exp2(scores).astype(BF16)
            acc[...] += jnp.dot(weights, values[pl.ds(at, block), :], preferred_element_type=F32)

        @pl.when(safe)
        def _():
            def body(i, carry):
                at = place_of(i)
                add_plain(at, scores_of(at))
                return carry

            lax.fori_loop(0, total, body, 0)
            at = pl.multiple_of(full * block, block)
            add_plain(at, jnp.where(at + column <= token, scores_of(at), lowest_score))

        @pl.when(jnp.logical_not(safe))
        def _():
            top[...] = jnp.full_like(top, lowest_score)

            def body(i, carry):
                last = i == total
                at = jnp.where(last, pl.multiple_of(full * block, block), place_of(i))
                at = pl.multiple_of(at, block)
                entry = jnp.where(last, at, -block) + column
                scores = jnp.where(entry <= token, scores_of(at), lowest_score)
                before = top[...]
                now = jnp.maximum(before, jnp.max(scores, axis=1, keepdims=True))
                factor = jnp.exp2(before - now)
                weights = jnp.exp2(scores - now[:, :1]).astype(BF16)
                fresh = jnp.dot(weights, values[pl.ds(at, block), :], preferred_element_type=F32)
                acc[...] = acc[...] * jnp.concatenate([factor, factor], axis=1) + fresh
                top[...] = now
                return carry

            lax.fori_loop(0, total + 1, body, 0)

        for g in range(group):
            part = slice(g * rows, (g + 1) * rows)
            o_ref[0, :, g * head : (g + 1) * head] = (acc[part, :head] / acc[part, head:]).astype(BF16)

    grid_spec = pltpu.PrefetchScalarGridSpec(
        num_scalar_prefetch=2,
        grid=(count,),
        in_specs=[
            pl.BlockSpec((1, rows, width), lambda i, meta, size: (meta[1] + i * stride, 0, 0)),
            pl.BlockSpec(memory_space=pltpu.VMEM),
        ],
        out_specs=pl.BlockSpec((1, rows, width), lambda i, meta, size: (i, 0, 0)),
        scratch_shapes=[
            pltpu.VMEM((capacity, head), BF16),
            pltpu.VMEM((capacity, pair), BF16),
            pltpu.VMEM((stack, head), BF16),
            pltpu.VMEM((stack, pair), F32),
            pltpu.VMEM((stack, head), F32),
            pltpu.VMEM((1, head), F32),
            pltpu.SMEM((1,), jnp.int32),
            pltpu.SMEM((1,), F32),
        ],
    )
    return pl.pallas_call(
        kernel,
        grid_spec=grid_spec,
        out_shape=jax.ShapeDtypeStruct((count, rows, width), BF16),
        compiler_params=pltpu.CompilerParams(vmem_limit_bytes=60 << 20),
        name="attend",
    )(jnp.stack([j, jnp.int32(start)]).astype(jnp.int32), lengths, queries, entries)


def project(rotated, entries, lengths, out_weight, j, nz, nj, nt):
    groups = nz // nt
    rows, columns = rotated.shape[1], out_weight.shape[1]
    tp = lax.axis_index("tp")
    entries, out_weight = lax.optimization_barrier((entries, out_weight))
    swaps = [[(i, i ^ r) for i in range(nj)] for r in range(nj)]
    weights = [out_weight]
    for r in range(1, nj):
        weights.append(lax.ppermute(out_weight, "j", swaps[r]))
    wide = []
    for g in range(groups):
        part = attend(rotated, entries, lengths, j, g, groups)
        wide.append(lax.all_gather(part, "z", axis=2, tiled=True))
    out = jnp.zeros((groups, nj, rows, columns), BF16)
    ready = []
    for g in range(groups):
        wide[g], ready = lax.optimization_barrier((wide[g], ready))
        for r in [0] + list(range(1, nj)):
            partial = jnp.einsum("ctk,kn->ctn", wide[g], weights[r], preferred_element_type=F32)
            total = lax.dynamic_index_in_dim(partial, tp, 0, keepdims=False)
            for step in range(1, nt):
                turn = [(i, (i + step) % nt) for i in range(nt)]
                away = lax.dynamic_index_in_dim(partial, (tp + step) % nt, 0, keepdims=False)
                total = total + lax.ppermute(away.astype(BF16), "tp", turn).astype(F32)
            total = total.astype(BF16)
            ready.append(total[:1, :1])
            if r:
                total = lax.ppermute(total, "j", swaps[r])
            out = lax.dynamic_update_slice(out, total[None, None], (g, j ^ r, 0, 0))
    return out.reshape(groups * nj * rows, columns)


def body(queries, span_kv, cache_kv, out_weight, offset, lengths, *, nz, nj, nt):
    rows, width = queries.shape
    kv_local, head = span_kv.shape[1], span_kv.shape[3]
    cached = cache_kv.shape[0]
    z = lax.axis_index("z")
    j = lax.axis_index("j")
    positions = offset[0] + (z * nj + j) * rows + jnp.arange(rows, dtype=jnp.int32)

    span_keys = rotate(span_kv[:, :, 0, :].astype(F32), positions).astype(BF16)
    span_part = jnp.concatenate([span_keys, span_kv[:, :, 1, :]], axis=-1)
    cache_part = cache_kv.reshape(cached, kv_local, 2 * head)
    local = jnp.concatenate([cache_part, span_part], axis=0).transpose(1, 0, 2)
    rotated = rotate(queries.reshape(rows, width // head, head).astype(F32), positions)
    rotated = rotated.astype(BF16).reshape(rows, kv_local, width // kv_local).transpose(1, 0, 2)
    if nz > 1:
        local = lax.all_to_all(local, "z", 0, 0, tiled=True)
        rotated = lax.all_to_all(rotated, "z", 0, 0, tiled=True)
    entries = lax.all_gather(local, "j", axis=0, tiled=False)
    if nz % nt == 0 and nj & (nj - 1) == 0:
        return project(rotated, entries, lengths, out_weight, j, nz, nj, nt)
    attention = attend(rotated, entries, lengths, j, 0, 1)
    wide = attention.reshape(nz * rows, -1)
    wide = lax.all_gather(wide, ("z", "j"), axis=0, tiled=True)
    projected = jnp.dot(wide, out_weight, preferred_element_type=F32).astype(BF16)
    return lax.psum_scatter(projected, "tp", scatter_dimension=0, tiled=True)


def solution(mesh):
    nc, nt = mesh.shape["ctx"], mesh.shape["tp"]

    def run(queries, span_kv, cache_kv, out_weight, offset, lengths):
        kv_local = span_kv.shape[1] // nt
        nz = kv_local
        nj = nc // nz
        inner = Mesh(mesh.devices.reshape(nz, nj, nt), ("z", "j", "tp"))
        ctx = ("z", "j")
        call = jax.shard_map(
            functools.partial(body, nz=nz, nj=nj, nt=nt),
            mesh=inner,
            in_specs=(
                P(ctx, "tp"),
                P(ctx, "tp", None, None),
                P(ctx, "tp", None, None),
                P("tp", ctx),
                P(),
                P(),
            ),
            out_specs=P("tp", ctx),
            check_vma=False,
        )
        return call(queries, span_kv, cache_kv, out_weight, offset, lengths)

    return run
```

```python
import functools
import math

import jax
import jax.numpy as jnp
from jax import lax
from jax.experimental import pallas as pl
from jax.experimental.pallas import tpu as pltpu
from jax.sharding import Mesh
from jax.sharding import PartitionSpec as P


F32 = jnp.float32
BF16 = jnp.bfloat16
lowest_score = -1e30
rope_base = 500000.0
bound_limit = 90.0
key_rows = 512


def rotate(values, positions):
    head_size = values.shape[-1]
    half_dim = head_size // 2
    frequency = jnp.exp(
        jnp.arange(half_dim, dtype=F32) * (-2.0 * math.log(rope_base) / head_size)
    )
    angles = positions.astype(F32)[:, None] * frequency[None, :]
    cosine = jnp.cos(angles)[:, None, :]
    sine_part = jnp.sin(angles)[:, None, :]
    first_half = values[..., :half_dim]
    second_half = values[..., half_dim:]
    return jnp.concatenate(
        [
            first_half * cosine - second_half * sine_part,
            second_half * cosine + first_half * sine_part,
        ],
        axis=-1,
    )


def square_bound(rows):
    squares = rows * rows
    ones = jnp.ones((rows.shape[1], rows.shape[1]), BF16)
    sums = jnp.dot(squares, ones, preferred_element_type=F32)
    return jnp.max(sums, axis=0, keepdims=True)


def attend(queries, entries, lengths, j, start, stride, count):
    _, rows, width = queries.shape
    nj, nz, local, pair = entries.shape
    cached = local - rows
    head = pair // 2
    group = width // head
    shards = nj * nz
    slots = lengths.shape[0]
    slot = cached * shards // slots
    per_shard = cached // slot
    span = shards * rows
    block = key_rows
    span_blocks = span // block
    stack = group * rows
    slice_rows = min(stack, 512)
    slow_rows = min(stack, 256)
    scale = math.log2(math.e) / math.sqrt(head)
    capacity = span + shards * cached + block

    def kernel(meta_ref, len_ref, q_ref, kv_ref, o_ref, keys, values, stacked, acc, top, norms, counts, bounds):
        step = pl.program_id(0)

        @pl.when(step == 0)
        def _():
            norms[...] = jnp.zeros_like(norms)

            def put_span(shard, carry):
                place = pl.ds(pl.multiple_of(shard * rows, rows), rows)
                piece = kv_ref[shard % nj, shard // nj, cached:, :]
                keys[place, :] = piece[:, :head]
                values[place, :head] = piece[:, head:]
                values[place, head:] = jnp.ones((rows, head), BF16)
                norms[...] = jnp.maximum(norms[...], square_bound(piece[:, :head]))
                return carry

            lax.fori_loop(0, shards, put_span, 0)
            index = lax.broadcasted_iota(jnp.int32, (slot, head), 0)

            def put_slot(number, at):
                shard = number // per_shard
                inside = pl.multiple_of((number % per_shard) * slot, slot)
                piece = kv_ref[shard % nj, shard // nj, pl.ds(inside, slot), :]
                size = len_ref[number]
                place = pl.ds(pl.multiple_of(at, 16), slot)
                keys[place, :] = piece[:, :head]
                values[place, :head] = piece[:, head:]
                values[place, head:] = jnp.where(index < size, 1.0, 0.0).astype(BF16)
                norms[...] = jnp.maximum(norms[...], square_bound(piece[:, :head]))
                return at + (size + 15) // 16 * 16

            end = lax.fori_loop(0, slots, put_slot, span)
            place = pl.ds(pl.multiple_of(end, 16), block)
            keys[place, :] = jnp.broadcast_to(kv_ref[0, 0, 0:1, :head], (block, head))
            values[place, :] = jnp.zeros((block, pair), BF16)
            counts[0] = (end - span + block - 1) // block
            bounds[0] = jnp.max(norms[...])

        for g in range(group):
            stacked[g * rows : (g + 1) * rows, :] = q_ref[0, :, g * head : (g + 1) * head]
        acc[...] = jnp.zeros_like(acc)
        first_token = (meta_ref[0] + (meta_ref[1] + step * stride) * nj) * rows
        full = first_token // block
        total = full + counts[0]
        query_bound = jnp.max(square_bound(stacked[...]))
        safe = query_bound * bounds[0] * (1.03 * scale * scale) <= bound_limit * bound_limit

        def scores_of(at, part):
            raw = lax.dot_general(
                stacked[part, :],
                keys[pl.ds(at, block), :],
                (((1,), (1,)), ((), ())),
                preferred_element_type=F32,
            )
            return raw * scale

        def masked_of(at, part, first):
            token = first_token + (first + lax.broadcasted_iota(jnp.int32, (slice_rows, block), 0)) % rows
            column = lax.broadcasted_iota(jnp.int32, (slice_rows, block), 1)
            return jnp.where(at + column <= token, scores_of(at, part), lowest_score)

        def place_of(i):
            return pl.multiple_of(jnp.where(i < full, i, span_blocks + i - full) * block, block)

        def part_of(n, size):
            first = pl.multiple_of(n * size, size)
            return pl.ds(first, size), first

        last = pl.multiple_of(full * block, block)

        def add_plain(at, part, scores):
            weights = jnp.exp2(scores).astype(BF16)
            acc[part, :] += jnp.dot(weights, values[pl.ds(at, block), :], preferred_element_type=F32)

        @pl.when(safe)
        def _():
            def body(i, carry):
                at = place_of(i)
                whole = slice(0, stack)
                add_plain(at, whole, scores_of(at, whole))
                return carry

            lax.fori_loop(0, total, body, 0)

            def edge(n, carry):
                part, first = part_of(n, slice_rows)
                add_plain(last, part, masked_of(last, part, first))
                return carry

            lax.fori_loop(0, stack // slice_rows, edge, 0)

        @pl.when(jnp.logical_not(safe))
        def _():
            top[...] = jnp.full_like(top, lowest_score)

            def add_online(at, part, scores):
                before = top[part, :]
                now = jnp.maximum(before, jnp.max(scores, axis=1, keepdims=True))
                factor = jnp.exp2(before - now)
                weights = jnp.exp2(scores - now[:, :1]).astype(BF16)
                fresh = jnp.dot(weights, values[pl.ds(at, block), :], preferred_element_type=F32)
                acc[part, :] = acc[part, :] * jnp.concatenate([factor, factor], axis=1) + fresh
                top[part, :] = now

            def rows_body(n, carry):
                part, first = part_of(n, slow_rows)

                def body(i, inner):
                    edge_block = i == total
                    at = pl.multiple_of(jnp.where(edge_block, last, place_of(i)), block)
                    token = first_token + (first + lax.broadcasted_iota(jnp.int32, (slow_rows, block), 0)) % rows
                    column = lax.broadcasted_iota(jnp.int32, (slow_rows, block), 1)
                    entry = jnp.where(edge_block, last, -block) + column
                    add_online(at, part, jnp.where(entry <= token, scores_of(at, part), lowest_score))
                    return inner

                lax.fori_loop(0, total + 1, body, 0)
                return carry

            lax.fori_loop(0, stack // slow_rows, rows_body, 0)

        for g in range(group):
            part = slice(g * rows, (g + 1) * rows)
            o_ref[0, :, g * head : (g + 1) * head] = (acc[part, :head] / acc[part, head:]).astype(BF16)

    grid_spec = pltpu.PrefetchScalarGridSpec(
        num_scalar_prefetch=2,
        grid=(count,),
        in_specs=[
            pl.BlockSpec((1, rows, width), lambda i, meta, size: (meta[1] + i * stride, 0, 0)),
            pl.BlockSpec(memory_space=pltpu.VMEM),
        ],
        out_specs=pl.BlockSpec((1, rows, width), lambda i, meta, size: (i, 0, 0)),
        scratch_shapes=[
            pltpu.VMEM((capacity, head), BF16),
            pltpu.VMEM((capacity, pair), BF16),
            pltpu.VMEM((stack, head), BF16),
            pltpu.VMEM((stack, pair), F32),
            pltpu.VMEM((stack, head), F32),
            pltpu.VMEM((1, head), F32),
            pltpu.SMEM((1,), jnp.int32),
            pltpu.SMEM((1,), F32),
        ],
    )
    return pl.pallas_call(
        kernel,
        grid_spec=grid_spec,
        out_shape=jax.ShapeDtypeStruct((count, rows, width), BF16),
        compiler_params=pltpu.CompilerParams(vmem_limit_bytes=60 << 20),
        name="attend",
    )(jnp.stack([j, jnp.int32(start)]).astype(jnp.int32), lengths, queries, entries)


def project(rotated, entries, lengths, out_weight, j, nz, nt):
    nj = entries.shape[0]
    groups = nz // nt
    rows, columns = rotated.shape[1], out_weight.shape[1]
    half = out_weight.shape[0] // 2
    tp = lax.axis_index("tp")
    entries, out_weight = lax.optimization_barrier((entries, out_weight))
    near = move(1, out_weight)
    far = move(2, out_weight)
    pieces = []
    for g in range(groups):
        calls = [(owner, 1) for owner in reversed(range(nt))] if g < groups - 1 else [(0, nt)]
        for owner, count in calls:
            part = attend(rotated, entries, lengths, j, owner * groups + g, groups, count)
            pieces.append(lax.all_gather(part, "z", axis=2, tiled=True))
    across = (move(1, far[:half]), move(2, near[half:]))
    weights = [(out_weight,), (near,), (far,), across]

    def times(left, r):
        if len(weights[r]) == 1:
            return jnp.einsum("ctk,kn->ctn", left, weights[r][0], preferred_element_type=F32)
        first = jnp.einsum("ctk,kn->ctn", left[..., :half], weights[r][0], preferred_element_type=F32)
        return first + jnp.einsum("ctk,kn->ctn", left[..., half:], weights[r][1], preferred_element_type=F32)

    out = jnp.zeros((groups, nj, rows, columns), BF16)
    for g in range(groups):
        lefts = pieces[g * nt : (g + 1) * nt][::-1] if g < groups - 1 else pieces[g * nt :]
        for r in [0, 1, 2, 3] if g < groups - 1 else [3, 1, 2, 0]:
            parts = []
            for left in lefts:
                parts.append(times(left, r))
            chunks = jnp.concatenate(parts) if len(parts) > 1 else parts[0]
            total = lax.dynamic_index_in_dim(chunks, tp, 0, keepdims=False)
            for step in range(1, nt):
                turn = [(i, (i + step) % nt) for i in range(nt)]
                away = lax.dynamic_index_in_dim(chunks, (tp + step) % nt, 0, keepdims=False)
                away = lax.ppermute(away.astype(BF16), "tp", turn)
                total = total + away.astype(F32)
            total = total.astype(BF16)
            if r:
                total = move(r, total)
            out = lax.dynamic_update_slice(out, total[None, None], (g, j ^ r, 0, 0))
    return out.reshape(groups * nj * rows, columns)


def move(r, array):
    return lax.ppermute(array, "j", [(i, i ^ r) for i in range(4)])


def body(queries, span_kv, cache_kv, out_weight, offset, lengths, *, nz, nj, nt):
    rows, width = queries.shape
    kv_local, head = span_kv.shape[1], span_kv.shape[3]
    cached = cache_kv.shape[0]
    z = lax.axis_index("z")
    j = lax.axis_index("j")
    positions = offset[0] + (z * nj + j) * rows + jnp.arange(rows, dtype=jnp.int32)

    span_keys = rotate(span_kv[:, :, 0, :].astype(F32), positions).astype(BF16)
    span = jnp.concatenate([span_keys, span_kv[:, :, 1, :]], axis=-1)
    slots = lengths.shape[0] // (nz * nj)
    sizes = lax.dynamic_slice_in_dim(lengths, (z * nj + j) * slots, slots)
    cache = cache_kv.reshape(slots, cached // slots, kv_local, 2 * head)
    inside = jnp.arange(cached // slots, dtype=jnp.int32)
    valid = (inside[None, :] < sizes[:, None])[:, :, None, None]
    is_key = jnp.arange(2 * head, dtype=jnp.int32) < head
    filler = jnp.where(is_key, cache[:, :1], jnp.zeros((), BF16))
    cache = jnp.where(valid, cache, filler).reshape(cached, kv_local, 2 * head)
    local = jnp.concatenate([cache, span], axis=0).transpose(1, 0, 2)
    rotated = rotate(queries.reshape(rows, width // head, head).astype(F32), positions)
    rotated = rotated.astype(BF16).reshape(rows, kv_local, width // kv_local).transpose(1, 0, 2)
    split = nz % nt == 0 and nj == 4
    if nz > 1:
        local = lax.all_to_all(local, "z", 0, 0, tiled=True)
        rotated, local = lax.optimization_barrier((rotated, local))
        rotated = lax.all_to_all(rotated, "z", 0, 0, tiled=True)
    entries = lax.all_gather(local, "j", axis=0, tiled=False)

    if split:
        return project(rotated, entries, lengths, out_weight, j, nz, nt)
    attention = attend(rotated, entries, lengths, j, 0, 1, nz)
    wide = attention.reshape(nz * rows, -1)
    wide = lax.all_gather(wide, ("z", "j"), axis=0, tiled=True)
    projected = jnp.dot(wide, out_weight, preferred_element_type=F32).astype(BF16)
    return lax.psum_scatter(projected, "tp", scatter_dimension=0, tiled=True)


def solution(mesh):
    nc, nt = mesh.shape["ctx"], mesh.shape["tp"]

    def run(queries, span_kv, cache_kv, out_weight, offset, lengths):
        kv_local = span_kv.shape[1] // nt
        nz = kv_local
        nj = nc // nz
        inner = Mesh(mesh.devices.reshape(nz, nj, nt), ("z", "j", "tp"))
        ctx = ("z", "j")
        call = jax.shard_map(
            functools.partial(body, nz=nz, nj=nj, nt=nt),
            mesh=inner,
            in_specs=(
                P(ctx, "tp"),
                P(ctx, "tp", None, None),
                P(ctx, "tp", None, None),
                P("tp", ctx),
                P(),
                P(),
            ),
            out_specs=P("tp", ctx),
            check_vma=False,
        )
        return call(queries, span_kv, cache_kv, out_weight, offset, lengths)

    return run
```

```python
import functools
import math

import jax
import jax.numpy as jnp
from jax import lax
from jax.experimental import pallas as pl
from jax.experimental.pallas import tpu as pltpu
from jax.sharding import Mesh
from jax.sharding import PartitionSpec as P


F32 = jnp.float32
BF16 = jnp.bfloat16
lowest_score = -1e30
rope_base = 500000.0
bound_limit = 90.0
key_rows = 512


def rotate(values, positions):
    head_size = values.shape[-1]
    half_dim = head_size // 2
    frequency = jnp.exp(
        jnp.arange(half_dim, dtype=F32) * (-2.0 * math.log(rope_base) / head_size)
    )
    angles = positions.astype(F32)[:, None] * frequency[None, :]
    cosine = jnp.cos(angles)[:, None, :]
    sine_part = jnp.sin(angles)[:, None, :]
    first_half = values[..., :half_dim]
    second_half = values[..., half_dim:]
    return jnp.concatenate(
        [
            first_half * cosine - second_half * sine_part,
            second_half * cosine + first_half * sine_part,
        ],
        axis=-1,
    )


def square_bound(rows):
    squares = rows * rows
    ones = jnp.ones((rows.shape[1], rows.shape[1]), BF16)
    sums = jnp.dot(squares, ones, preferred_element_type=F32)
    return jnp.max(sums, axis=0, keepdims=True)


def attend(queries, key_parts, value_parts, ids, lengths, j, nj, start, stride, count):
    _, rows, width = queries.shape
    local, head = key_parts[0].shape[1:]
    cached = local - rows
    pair = 2 * head
    parts = len(key_parts)
    group = width // head
    shards = ids.shape[0]
    slots = lengths.shape[0]
    slot = cached * shards // slots
    per_shard = cached // slot
    span = shards * rows
    block = key_rows
    span_blocks = span // block
    stack = group * rows
    slice_rows = min(stack, 512)
    slow_rows = min(stack, 128)
    scale = math.log2(math.e) / math.sqrt(head)
    capacity = span + shards * cached + block

    def kernel(meta_ref, len_ref, q_ref, *refs):
        key_refs, value_refs = refs[:parts], refs[parts : 2 * parts]
        o_ref, staged, keys, values, stacked, acc, top, norms, counts, bounds, arrived = refs[2 * parts :]
        step = pl.program_id(0)

        @pl.when(step == 0)
        def _():
            norms[...] = jnp.zeros_like(norms)

            index = lax.broadcasted_iota(jnp.int32, (slot, head), 0)
            copies = []
            for which, pieces in enumerate((key_refs, value_refs)):
                base = 0
                for piece in pieces:
                    size = piece.shape[0]
                    copies.append(
                        pltpu.make_async_copy(
                            piece, staged.at[which, pl.ds(base, size)], arrived.at[len(copies)]
                        )
                    )
                    base += size
            for copy in copies:
                copy.start()
            for copy in copies:
                copy.wait()

            def put_shard(n, at):
                shard = meta_ref[2 + n]
                place = pl.ds(pl.multiple_of(shard * rows, rows), rows)
                piece = staged[0, n, cached:, :]
                keys[place, :] = piece
                values[place, :head] = staged[1, n, cached:, :]
                values[place, head:] = jnp.ones((rows, head), BF16)
                norms[...] = jnp.maximum(norms[...], square_bound(piece))
                for k in range(per_shard):
                    piece = staged[0, n, k * slot : (k + 1) * slot, :]
                    size = len_ref[shard * per_shard + k]
                    place = pl.ds(pl.multiple_of(at, 16), slot)
                    keys[place, :] = piece
                    values[place, :head] = staged[1, n, k * slot : (k + 1) * slot, :]
                    values[place, head:] = jnp.where(index < size, 1.0, 0.0).astype(BF16)
                    norms[...] = jnp.maximum(norms[...], square_bound(piece))
                    at = at + (size + 15) // 16 * 16
                return at

            end = lax.fori_loop(0, shards, put_shard, jnp.int32(span))
            place = pl.ds(pl.multiple_of(end, 16), block)
            keys[place, :] = jnp.broadcast_to(staged[0, 0, 0:1, :], (block, head))
            values[place, :] = jnp.zeros((block, pair), BF16)
            counts[0] = (end - span + block - 1) // block
            bounds[0] = jnp.max(norms[...])

        for g in range(group):
            stacked[g * rows : (g + 1) * rows, :] = q_ref[0, :, g * head : (g + 1) * head]
        acc[...] = jnp.zeros_like(acc)
        first_token = (meta_ref[0] + (meta_ref[1] + step * stride) * nj) * rows
        full = first_token // block
        total = full + counts[0]
        query_bound = jnp.max(square_bound(stacked[...]))
        safe = query_bound * bounds[0] * (1.03 * scale * scale) <= bound_limit * bound_limit

        def scores_of(at, part):
            raw = lax.dot_general(
                stacked[part, :],
                keys[pl.ds(at, block), :],
                (((1,), (1,)), ((), ())),
                preferred_element_type=F32,
            )
            return raw * scale

        def masked_of(at, part, first):
            token = first_token + (first + lax.broadcasted_iota(jnp.int32, (slice_rows, block), 0)) % rows
            column = lax.broadcasted_iota(jnp.int32, (slice_rows, block), 1)
            return jnp.where(at + column <= token, scores_of(at, part), lowest_score)

        def place_of(i):
            return pl.multiple_of(jnp.where(i < full, i, span_blocks + i - full) * block, block)

        def part_of(n, size):
            first = pl.multiple_of(n * size, size)
            return pl.ds(first, size), first

        last = pl.multiple_of(full * block, block)

        def add_plain(at, part, scores):
            weights = jnp.exp2(scores).astype(BF16)
            acc[part, :] += jnp.dot(weights, values[pl.ds(at, block), :], preferred_element_type=F32)

        @pl.when(safe)
        def _():
            def body(i, carry):
                at = place_of(i)
                whole = slice(0, stack)
                add_plain(at, whole, scores_of(at, whole))
                return carry

            lax.fori_loop(0, total, body, 0)

            def edge(n, carry):
                part, first = part_of(n, slice_rows)
                add_plain(last, part, masked_of(last, part, first))
                return carry

            lax.fori_loop(0, stack // slice_rows, edge, 0)

        @pl.when(jnp.logical_not(safe))
        def _():
            top[...] = jnp.full_like(top, lowest_score)

            def add_online(at, part, scores):
                before = top[part, :]
                now = jnp.maximum(before, jnp.max(scores, axis=1, keepdims=True))
                factor = jnp.exp2(before - now)
                weights = jnp.exp2(scores - now[:, :1]).astype(BF16)
                fresh = jnp.dot(weights, values[pl.ds(at, block), :], preferred_element_type=F32)
                acc[part, :] = acc[part, :] * jnp.concatenate([factor, factor], axis=1) + fresh
                top[part, :] = now

            def rows_body(n, carry):
                part, first = part_of(n, slow_rows)

                def body(i, inner):
                    edge_block = i == total
                    at = pl.multiple_of(jnp.where(edge_block, last, place_of(i)), block)
                    token = first_token + (first + lax.broadcasted_iota(jnp.int32, (slow_rows, block), 0)) % rows
                    column = lax.broadcasted_iota(jnp.int32, (slow_rows, block), 1)
                    entry = jnp.where(edge_block, last, -block) + column
                    add_online(at, part, jnp.where(entry <= token, scores_of(at, part), lowest_score))
                    return inner

                lax.fori_loop(0, total + 1, body, 0)
                return carry

            lax.fori_loop(0, stack // slow_rows, rows_body, 0)

        for g in range(group):
            part = slice(g * rows, (g + 1) * rows)
            o_ref[0, :, g * head : (g + 1) * head] = (acc[part, :head] / acc[part, head:]).astype(BF16)

    meta = jnp.concatenate([jnp.stack([j, jnp.int32(start)]).astype(jnp.int32), ids])
    grid_spec = pltpu.PrefetchScalarGridSpec(
        num_scalar_prefetch=2,
        grid=(count,),
        in_specs=[
            pl.BlockSpec((1, rows, width), lambda i, meta, size: (meta[1] + i * stride, 0, 0)),
        ]
        + [pl.BlockSpec(memory_space=pl.ANY)] * (2 * parts),
        out_specs=pl.BlockSpec((1, rows, width), lambda i, meta, size: (i, 0, 0)),
        scratch_shapes=[
            pltpu.VMEM((2, shards, local, head), BF16),
            pltpu.VMEM((capacity, head), BF16),
            pltpu.VMEM((capacity, pair), BF16),
            pltpu.VMEM((stack, head), BF16),
            pltpu.VMEM((stack, pair), F32),
            pltpu.VMEM((stack, head), F32),
            pltpu.VMEM((1, head), F32),
            pltpu.SMEM((1,), jnp.int32),
            pltpu.SMEM((1,), F32),
            pltpu.SemaphoreType.DMA((2 * parts,)),
        ],
    )
    return pl.pallas_call(
        kernel,
        grid_spec=grid_spec,
        out_shape=jax.ShapeDtypeStruct((count, rows, width), BF16),
        compiler_params=pltpu.CompilerParams(vmem_limit_bytes=60 << 20),
        name="attend",
    )(meta, lengths, queries, *key_parts, *value_parts)


def project(rotated, key_parts, value_parts, ids, lengths, out_weight, j, nz, nj, nt):
    groups = nz // nt
    rows, columns = rotated.shape[1], out_weight.shape[1]
    half = out_weight.shape[0] // 2
    tp = lax.axis_index("tp")
    key_parts, value_parts, out_weight = lax.optimization_barrier((key_parts, value_parts, out_weight))
    near = move(1, out_weight)
    far = move(2, out_weight)
    pieces = []
    for g in range(groups):
        calls = [(owner, 1) for owner in reversed(range(nt))] if g < groups - 1 else [(0, nt)]
        for owner, count in calls:
            first = owner * groups + g
            part = attend(rotated, key_parts, value_parts, ids, lengths, j, nj, first, groups, count)
            pieces.append(lax.all_gather(part, "z", axis=2, tiled=True))
    across = (move(1, far[:half]), move(2, near[half:]))
    weights = [(out_weight,), (near,), (far,), across]

    def times(left, r):
        if len(weights[r]) == 1:
            return jnp.einsum("ctk,kn->ctn", left, weights[r][0], preferred_element_type=F32)
        first = jnp.einsum("ctk,kn->ctn", left[..., :half], weights[r][0], preferred_element_type=F32)
        return first + jnp.einsum("ctk,kn->ctn", left[..., half:], weights[r][1], preferred_element_type=F32)

    out = jnp.zeros((groups, nj, rows, columns), BF16)
    for g in range(groups):
        lefts = pieces[g * nt : (g + 1) * nt][::-1] if g < groups - 1 else pieces[g * nt :]
        for r in [0, 1, 2, 3] if g < groups - 1 else [3, 1, 2, 0]:
            parts = []
            for left in lefts:
                parts.append(times(left, r))
            chunks = jnp.concatenate(parts) if len(parts) > 1 else parts[0]
            total = lax.dynamic_index_in_dim(chunks, tp, 0, keepdims=False)
            for step in range(1, nt):
                turn = [(i, (i + step) % nt) for i in range(nt)]
                away = lax.dynamic_index_in_dim(chunks, (tp + step) % nt, 0, keepdims=False)
                away = lax.ppermute(away.astype(BF16), "tp", turn)
                total = total + away.astype(F32)
            total = total.astype(BF16)
            if r:
                total = move(r, total)
            out = lax.dynamic_update_slice(out, total[None, None], (g, j ^ r, 0, 0))
    return out.reshape(groups * nj * rows, columns)


def spread(own):
    half = own.shape[0] // 2
    near, far = move(1, own), move(2, own)
    return [own, near, far, move(1, far[:half]), move(2, near[half:])]


def move(r, array):
    return lax.ppermute(array, "j", [(i, i ^ r) for i in range(4)])


def body(queries, span_kv, cache_kv, out_weight, offset, lengths, *, nz, nj, nt):
    rows, width = queries.shape
    kv_local, head = span_kv.shape[1], span_kv.shape[3]
    cached = cache_kv.shape[0]
    z = lax.axis_index("z")
    j = lax.axis_index("j")
    positions = offset[0] + (z * nj + j) * rows + jnp.arange(rows, dtype=jnp.int32)

    span_keys = rotate(span_kv[:, :, 0, :].astype(F32), positions).astype(BF16)
    span = jnp.concatenate([span_keys, span_kv[:, :, 1, :]], axis=-1)
    slots = lengths.shape[0] // (nz * nj)
    sizes = lax.dynamic_slice_in_dim(lengths, (z * nj + j) * slots, slots)
    cache = cache_kv.reshape(slots, cached // slots, kv_local, 2 * head)
    inside = jnp.arange(cached // slots, dtype=jnp.int32)
    valid = (inside[None, :] < sizes[:, None])[:, :, None, None]
    is_key = jnp.arange(2 * head, dtype=jnp.int32) < head
    filler = jnp.where(is_key, cache[:, :1], jnp.zeros((), BF16))
    cache = jnp.where(valid, cache, filler).reshape(cached, kv_local, 2 * head)
    local = jnp.concatenate([cache, span], axis=0).transpose(1, 0, 2)
    rotated = rotate(queries.reshape(rows, width // head, head).astype(F32), positions)
    rotated = rotated.astype(BF16).reshape(rows, kv_local, width // kv_local).transpose(1, 0, 2)
    split = nz % nt == 0 and nj == 4 and nz % 2 == 0
    keys, values = local[..., :head], local[..., head:]
    if nz > 1:
        keys = lax.all_to_all(keys, "z", 0, 0, tiled=True)
        values, keys = lax.optimization_barrier((values, keys))
        values = lax.all_to_all(values, "z", 0, 0, tiled=True)
        rotated, values = lax.optimization_barrier((rotated, values))
        rotated = lax.all_to_all(rotated, "z", 0, 0, tiled=True)
    every = jnp.arange(nz, dtype=jnp.int32) * nj
    if split:
        ids = jnp.concatenate([every + j, every + (j ^ 1), every + (j ^ 2), every + (j ^ 3)]).astype(jnp.int32)
        key_parts, value_parts = spread(keys), spread(values)
        return project(rotated, key_parts, value_parts, ids, lengths, out_weight, j, nz, nj, nt)
    ids = (jnp.arange(nj, dtype=jnp.int32)[:, None] + every[None, :]).reshape(-1)
    key_parts = [lax.all_gather(keys, "j", axis=0, tiled=True)]
    value_parts = [lax.all_gather(values, "j", axis=0, tiled=True)]
    attention = attend(rotated, key_parts, value_parts, ids, lengths, j, nj, 0, 1, nz)
    wide = attention.reshape(nz * rows, -1)
    wide = lax.all_gather(wide, ("z", "j"), axis=0, tiled=True)
    projected = jnp.dot(wide, out_weight, preferred_element_type=F32).astype(BF16)
    return lax.psum_scatter(projected, "tp", scatter_dimension=0, tiled=True)


def solution(mesh):
    nc, nt = mesh.shape["ctx"], mesh.shape["tp"]

    def run(queries, span_kv, cache_kv, out_weight, offset, lengths):
        kv_local = span_kv.shape[1] // nt
        nz = kv_local
        nj = nc // nz
        inner = Mesh(mesh.devices.reshape(nz, nj, nt), ("z", "j", "tp"))
        ctx = ("z", "j")
        call = jax.shard_map(
            functools.partial(body, nz=nz, nj=nj, nt=nt),
            mesh=inner,
            in_specs=(
                P(ctx, "tp"),
                P(ctx, "tp", None, None),
                P(ctx, "tp", None, None),
                P("tp", ctx),
                P(),
                P(),
            ),
            out_specs=P("tp", ctx),
            check_vma=False,
        )
        return call(queries, span_kv, cache_kv, out_weight, offset, lengths)

    return run
```

```python
import functools
import math

import jax
import jax.numpy as jnp
from jax import lax
from jax.experimental import pallas as pl
from jax.experimental.pallas import tpu as pltpu
from jax.sharding import Mesh
from jax.sharding import PartitionSpec as P


F32 = jnp.float32
BF16 = jnp.bfloat16
lowest_score = -1e30
rope_base = 500000.0
bound_limit = 90.0
key_rows = 512


def rotate(values, positions):
    head_size = values.shape[-1]
    half_dim = head_size // 2
    frequency = jnp.exp(
        jnp.arange(half_dim, dtype=F32) * (-2.0 * math.log(rope_base) / head_size)
    )
    angles = positions.astype(F32)[:, None] * frequency[None, :]
    cosine = jnp.cos(angles)[:, None, :]
    sine_part = jnp.sin(angles)[:, None, :]
    first_half = values[..., :half_dim]
    second_half = values[..., half_dim:]
    return jnp.concatenate(
        [
            first_half * cosine - second_half * sine_part,
            second_half * cosine + first_half * sine_part,
        ],
        axis=-1,
    )


def square_bound(rows):
    squares = rows * rows
    ones = jnp.ones((rows.shape[1], rows.shape[1]), BF16)
    sums = jnp.dot(squares, ones, preferred_element_type=F32)
    return jnp.max(sums, axis=0, keepdims=True)


def key_bound(key_parts):
    squares = [jnp.max(jnp.sum(jnp.square(part.astype(F32)), axis=-1)) for part in key_parts]
    return functools.reduce(jnp.maximum, squares)[None]


def attend(queries, key_parts, value_parts, bound, ids, lengths, j, nj, start, stride, count):
    _, rows, width = queries.shape
    local, head = key_parts[0].shape[1:]
    cached = local - rows
    pair = 2 * head
    parts = len(key_parts)
    group = width // head
    shards = ids.shape[0]
    slots = lengths.shape[0]
    slot = cached * shards // slots
    per_shard = cached // slot
    span = shards * rows
    block = key_rows
    span_blocks = span // block
    stack = group * rows
    slice_rows = min(stack, 512)
    slow_rows = min(stack, 128)
    scale = math.log2(math.e) / math.sqrt(head)
    capacity = span + shards * cached + block

    def kernel(meta_ref, len_ref, bound_ref, q_ref, *refs):
        key_refs, value_refs = refs[:parts], refs[parts : 2 * parts]
        o_ref, staged, keys, values, stacked, acc, top, counts, arrived = refs[2 * parts :]
        step = pl.program_id(0)

        @pl.when(step == 0)
        def _():
            index = lax.broadcasted_iota(jnp.int32, (slot, head), 0)
            copies = []
            for which, pieces in enumerate((key_refs, value_refs)):
                base = 0
                for piece in pieces:
                    size = piece.shape[0]
                    copies.append(
                        pltpu.make_async_copy(
                            piece, staged.at[which, pl.ds(base, size)], arrived.at[len(copies)]
                        )
                    )
                    base += size
            for copy in copies:
                copy.start()
            for copy in copies:
                copy.wait()

            def put_shard(n, at):
                shard = meta_ref[2 + n]
                place = pl.ds(pl.multiple_of(shard * rows, rows), rows)
                keys[place, :] = staged[0, n, cached:, :]
                values[place, :head] = staged[1, n, cached:, :]
                values[place, head:] = jnp.ones((rows, head), BF16)
                for k in range(per_shard):
                    size = len_ref[shard * per_shard + k]
                    place = pl.ds(pl.multiple_of(at, 16), slot)
                    keys[place, :] = staged[0, n, k * slot : (k + 1) * slot, :]
                    values[place, :head] = staged[1, n, k * slot : (k + 1) * slot, :]
                    values[place, head:] = jnp.where(index < size, 1.0, 0.0).astype(BF16)
                    at = at + (size + 15) // 16 * 16
                return at

            end = lax.fori_loop(0, shards, put_shard, jnp.int32(span))
            place = pl.ds(pl.multiple_of(end, 16), block)
            keys[place, :] = jnp.broadcast_to(staged[0, 0, 0:1, :], (block, head))
            values[place, :] = jnp.zeros((block, pair), BF16)
            counts[0] = (end - span + block - 1) // block

        for g in range(group):
            stacked[g * rows : (g + 1) * rows, :] = q_ref[0, :, g * head : (g + 1) * head]
        acc[...] = jnp.zeros_like(acc)
        first_token = (meta_ref[0] + (meta_ref[1] + step * stride) * nj) * rows
        full = first_token // block
        total = full + counts[0]
        query_bound = jnp.max(square_bound(stacked[...]))
        safe = query_bound * bound_ref[0] * (1.03 * scale * scale) <= bound_limit * bound_limit

        def scores_of(at, part):
            raw = lax.dot_general(
                stacked[part, :],
                keys[pl.ds(at, block), :],
                (((1,), (1,)), ((), ())),
                preferred_element_type=F32,
            )
            return raw * scale

        def masked_of(at, part, first):
            token = first_token + (first + lax.broadcasted_iota(jnp.int32, (slice_rows, block), 0)) % rows
            column = lax.broadcasted_iota(jnp.int32, (slice_rows, block), 1)
            return jnp.where(at + column <= token, scores_of(at, part), lowest_score)

        def place_of(i):
            return pl.multiple_of(jnp.where(i < full, i, span_blocks + i - full) * block, block)

        def part_of(n, size):
            first = pl.multiple_of(n * size, size)
            return pl.ds(first, size), first

        last = pl.multiple_of(full * block, block)

        def add_plain(at, part, scores):
            weights = jnp.exp2(scores).astype(BF16)
            acc[part, :] += jnp.dot(weights, values[pl.ds(at, block), :], preferred_element_type=F32)

        @pl.when(safe)
        def _():
            def body(i, carry):
                at = place_of(i)
                whole = slice(0, stack)
                add_plain(at, whole, scores_of(at, whole))
                return carry

            lax.fori_loop(0, total, body, 0)

            def edge(n, carry):
                part, first = part_of(n, slice_rows)
                add_plain(last, part, masked_of(last, part, first))
                return carry

            lax.fori_loop(0, stack // slice_rows, edge, 0)

        @pl.when(jnp.logical_not(safe))
        def _():
            top[...] = jnp.full_like(top, lowest_score)

            def add_online(at, part, scores):
                before = top[part, :]
                now = jnp.maximum(before, jnp.max(scores, axis=1, keepdims=True))
                factor = jnp.exp2(before - now)
                weights = jnp.exp2(scores - now[:, :1]).astype(BF16)
                fresh = jnp.dot(weights, values[pl.ds(at, block), :], preferred_element_type=F32)
                acc[part, :] = acc[part, :] * jnp.concatenate([factor, factor], axis=1) + fresh
                top[part, :] = now

            def rows_body(n, carry):
                part, first = part_of(n, slow_rows)

                def body(i, inner):
                    edge_block = i == total
                    at = pl.multiple_of(jnp.where(edge_block, last, place_of(i)), block)
                    token = first_token + (first + lax.broadcasted_iota(jnp.int32, (slow_rows, block), 0)) % rows
                    column = lax.broadcasted_iota(jnp.int32, (slow_rows, block), 1)
                    entry = jnp.where(edge_block, last, -block) + column
                    add_online(at, part, jnp.where(entry <= token, scores_of(at, part), lowest_score))
                    return inner

                lax.fori_loop(0, total + 1, body, 0)
                return carry

            lax.fori_loop(0, stack // slow_rows, rows_body, 0)

        for g in range(group):
            part = slice(g * rows, (g + 1) * rows)
            o_ref[0, :, g * head : (g + 1) * head] = (acc[part, :head] / acc[part, head:]).astype(BF16)

    meta = jnp.concatenate([jnp.stack([j, jnp.int32(start)]).astype(jnp.int32), ids])
    grid_spec = pltpu.PrefetchScalarGridSpec(
        num_scalar_prefetch=2,
        grid=(count,),
        in_specs=[
            pl.BlockSpec(memory_space=pltpu.SMEM),
            pl.BlockSpec((1, rows, width), lambda i, meta, size: (meta[1] + i * stride, 0, 0)),
        ]
        + [pl.BlockSpec(memory_space=pl.ANY)] * (2 * parts),
        out_specs=pl.BlockSpec((1, rows, width), lambda i, meta, size: (i, 0, 0)),
        scratch_shapes=[
            pltpu.VMEM((2, shards, local, head), BF16),
            pltpu.VMEM((capacity, head), BF16),
            pltpu.VMEM((capacity, pair), BF16),
            pltpu.VMEM((stack, head), BF16),
            pltpu.VMEM((stack, pair), F32),
            pltpu.VMEM((stack, head), F32),
            pltpu.SMEM((1,), jnp.int32),
            pltpu.SemaphoreType.DMA((2 * parts,)),
        ],
    )
    return pl.pallas_call(
        kernel,
        grid_spec=grid_spec,
        out_shape=jax.ShapeDtypeStruct((count, rows, width), BF16),
        compiler_params=pltpu.CompilerParams(vmem_limit_bytes=60 << 20),
        name="attend",
    )(meta, lengths, bound, queries, *key_parts, *value_parts)


def project(rotated, key_parts, value_parts, bound, ids, lengths, out_weight, j, nz, nj, nt):
    groups = nz // nt
    rows, columns = rotated.shape[1], out_weight.shape[1]
    half = out_weight.shape[0] // 2
    tp = lax.axis_index("tp")
    key_parts, value_parts, out_weight = lax.optimization_barrier((key_parts, value_parts, out_weight))
    near = move(1, out_weight)
    far = move(2, out_weight)
    pieces = []
    for g in range(groups):
        calls = [(owner, 1) for owner in reversed(range(nt))] if g < groups - 1 else [(0, nt)]
        for owner, count in calls:
            first = owner * groups + g
            part = attend(rotated, key_parts, value_parts, bound, ids, lengths, j, nj, first, groups, count)
            pieces.append(lax.all_gather(part, "z", axis=2, tiled=True))
    across = (move(1, far[:half]), move(2, near[half:]))
    weights = [(out_weight,), (near,), (far,), across]

    def times(left, r):
        if len(weights[r]) == 1:
            return jnp.einsum("ctk,kn->ctn", left, weights[r][0], preferred_element_type=F32)
        first = jnp.einsum("ctk,kn->ctn", left[..., :half], weights[r][0], preferred_element_type=F32)
        return first + jnp.einsum("ctk,kn->ctn", left[..., half:], weights[r][1], preferred_element_type=F32)

    out = jnp.zeros((groups, nj, rows, columns), BF16)
    for g in range(groups):
        lefts = pieces[g * nt : (g + 1) * nt][::-1] if g < groups - 1 else pieces[g * nt :]
        for r in [0, 1, 2, 3] if g < groups - 1 else [3, 1, 2, 0]:
            parts = []
            for left in lefts:
                parts.append(times(left, r))
            chunks = jnp.concatenate(parts) if len(parts) > 1 else parts[0]
            total = lax.dynamic_index_in_dim(chunks, tp, 0, keepdims=False)
            for step in range(1, nt):
                turn = [(i, (i + step) % nt) for i in range(nt)]
                away = lax.dynamic_index_in_dim(chunks, (tp + step) % nt, 0, keepdims=False)
                away = lax.ppermute(away.astype(BF16), "tp", turn)
                total = total + away.astype(F32)
            total = total.astype(BF16)
            if r:
                total = move(r, total)
            out = lax.dynamic_update_slice(out, total[None, None], (g, j ^ r, 0, 0))
    return out.reshape(groups * nj * rows, columns)


def spread(own):
    half = own.shape[0] // 2
    near, far = move(1, own), move(2, own)
    return [own, near, far, move(1, far[:half]), move(2, near[half:])]


def move(r, array):
    return lax.ppermute(array, "j", [(i, i ^ r) for i in range(4)])


def body(queries, span_kv, cache_kv, out_weight, offset, lengths, *, nz, nj, nt):
    rows, width = queries.shape
    kv_local, head = span_kv.shape[1], span_kv.shape[3]
    cached = cache_kv.shape[0]
    z = lax.axis_index("z")
    j = lax.axis_index("j")
    positions = offset[0] + (z * nj + j) * rows + jnp.arange(rows, dtype=jnp.int32)

    span_keys = rotate(span_kv[:, :, 0, :].astype(F32), positions).astype(BF16)
    span = jnp.concatenate([span_keys, span_kv[:, :, 1, :]], axis=-1)
    slots = lengths.shape[0] // (nz * nj)
    sizes = lax.dynamic_slice_in_dim(lengths, (z * nj + j) * slots, slots)
    cache = cache_kv.reshape(slots, cached // slots, kv_local, 2 * head)
    inside = jnp.arange(cached // slots, dtype=jnp.int32)
    valid = (inside[None, :] < sizes[:, None])[:, :, None, None]
    is_key = jnp.arange(2 * head, dtype=jnp.int32) < head
    filler = jnp.where(is_key, cache[:, :1], jnp.zeros((), BF16))
    cache = jnp.where(valid, cache, filler).reshape(cached, kv_local, 2 * head)
    local = jnp.concatenate([cache, span], axis=0).transpose(1, 0, 2)
    rotated = rotate(queries.reshape(rows, width // head, head).astype(F32), positions)
    rotated = rotated.astype(BF16).reshape(rows, kv_local, width // kv_local).transpose(1, 0, 2)
    split = nz % nt == 0 and nj == 4 and nz % 2 == 0
    keys, values = local[..., :head], local[..., head:]
    if nz > 1:
        keys = lax.all_to_all(keys, "z", 0, 0, tiled=True)
        values, keys = lax.optimization_barrier((values, keys))
        values = lax.all_to_all(values, "z", 0, 0, tiled=True)
        rotated, values = lax.optimization_barrier((rotated, values))
        rotated = lax.all_to_all(rotated, "z", 0, 0, tiled=True)
    every = jnp.arange(nz, dtype=jnp.int32) * nj
    if split:
        ids = jnp.concatenate([every + j, every + (j ^ 1), every + (j ^ 2), every + (j ^ 3)]).astype(jnp.int32)
        key_parts, value_parts = spread(keys), spread(values)
        return project(rotated, key_parts, value_parts, key_bound(key_parts), ids, lengths, out_weight, j, nz, nj, nt)
    ids = (jnp.arange(nj, dtype=jnp.int32)[:, None] + every[None, :]).reshape(-1)
    key_parts = [lax.all_gather(keys, "j", axis=0, tiled=True)]
    value_parts = [lax.all_gather(values, "j", axis=0, tiled=True)]
    attention = attend(rotated, key_parts, value_parts, key_bound(key_parts), ids, lengths, j, nj, 0, 1, nz)
    wide = attention.reshape(nz * rows, -1)
    wide = lax.all_gather(wide, ("z", "j"), axis=0, tiled=True)
    projected = jnp.dot(wide, out_weight, preferred_element_type=F32).astype(BF16)
    return lax.psum_scatter(projected, "tp", scatter_dimension=0, tiled=True)


def solution(mesh):
    nc, nt = mesh.shape["ctx"], mesh.shape["tp"]

    def run(queries, span_kv, cache_kv, out_weight, offset, lengths):
        kv_local = span_kv.shape[1] // nt
        nz = kv_local
        nj = nc // nz
        inner = Mesh(mesh.devices.reshape(nz, nj, nt), ("z", "j", "tp"))
        ctx = ("z", "j")
        call = jax.shard_map(
            functools.partial(body, nz=nz, nj=nj, nt=nt),
            mesh=inner,
            in_specs=(
                P(ctx, "tp"),
                P(ctx, "tp", None, None),
                P(ctx, "tp", None, None),
                P("tp", ctx),
                P(),
                P(),
            ),
            out_specs=P("tp", ctx),
            check_vma=False,
        )
        return call(queries, span_kv, cache_kv, out_weight, offset, lengths)

    return run
```
